256 devices in a mesh: frames: 32 (over y, z_lo, x), space: 8 (over z_hi, core).
Axes of the slice: x: 4, y: 4, z: 8 (z_hi: 4, z_lo: 2; z = z_hi * 2 + z_lo), core: 2. Of those that a mesh axis runs over, the one named last changes fastest.
Arguments:
- latents: bfloat16 [32, 3584, 1152], P('frames', 'space'), may hold values from -6 to 6
- merge_slot: int32 [32, 3584], P('frames', 'space'), may hold values from 0 to 1791, as said below
- modulation: float32 [6, 1152], replicated, may hold values from -3 to 3
- spatial_qkv: bfloat16 [1152, 1728], replicated, may hold values from -0.41247896 to 0.41247896
- spatial_proj: bfloat16 [576, 1152], replicated, may hold values from -0.25 to 0.25
- temporal_qkv: bfloat16 [1152, 1728], replicated, may hold values from -0.41247896 to 0.41247896
- temporal_proj: bfloat16 [576, 1152], replicated, may hold values from -0.25 to 0.25
Outputs:
- block_out: bfloat16 [32, 3584, 1152], P('frames', 'space')
The draws below stay inside these ranges and needn't reach their ends.
Inputs may be any that keep to these rules, and one draw needn't show every extreme that they name: `merge_slot`: within each frame, the tokens of the k-th aligned block of 448 tokens join merged tokens k * 224 to (k + 1) * 224 - 1 only, and every merged token is joined by at least one token.
All inputs are finite; a program needn't handle non-finite values.
Results may differ from the reference program's by a relative error of at most 0.0062.
Values may be sent and summed in bfloat16 or wider, within the bound.
A program may use at most 128 MiB of HBM per device.

```python
import math
import jax
import jax.numpy as jnp
from jax import lax

D = 1152
HEADS = 8
HD = 72
ROWS = 448
INNER = 576
FRAMES = 32
TOK = 3584
HALF = 1792
MROWS = 224


def draw_projection(key, fan_rows, inner):
    base_key = jax.random.fold_in(key, 0)
    return jnp.clip(jax.random.normal(base_key, (fan_rows, 3 * inner), jnp.float32), -4.0, 4.0) / math.sqrt(fan_rows)


def draw_spatial_qkv(key, part):
    return draw_projection(jax.random.fold_in(key, 11), D, INNER).astype(jnp.bfloat16)


def draw_temporal_qkv(key, part):
    return draw_projection(jax.random.fold_in(key, 23), D, INNER).astype(jnp.bfloat16)


def draw_merge_slot(key, part):
    block_count = FRAMES * (TOK // ROWS)
    keys_all = jax.random.split(key, block_count)

    def one_block(block_key):
        order_key, extra_key = jax.random.split(block_key)
        order = jax.random.permutation(order_key, ROWS)
        extra = jax.random.randint(extra_key, (ROWS,), 0, MROWS)
        ranks = jnp.arange(ROWS, dtype=jnp.int32)
        slot_of_rank = jnp.where(ranks < MROWS, ranks, extra).astype(jnp.int32)
        return jnp.zeros((ROWS,), jnp.int32).at[order].set(slot_of_rank)
    local = jax.vmap(one_block)(keys_all).reshape(FRAMES, TOK // ROWS, ROWS)
    offsets = (jnp.arange(TOK // ROWS, dtype=jnp.int32) * MROWS)[None, :, None]
    return (local + offsets).reshape(FRAMES, TOK).astype(jnp.int32)


def steps_of(stream_key, extent, cuts, low, high):
    level = 1.0
    for axis_at, shards_of in cuts:
        heights = jax.random.uniform(jax.random.fold_in(jax.random.fold_in(stream_key, 6), axis_at), (shards_of,), jnp.float32, low / len(cuts), high / len(cuts))
        level = level * jnp.repeat(jnp.exp(heights), extent[axis_at] // shards_of).reshape((-1,) + (1,) * (len(extent) - 1 - axis_at))
    return level


def gaussian(own_key, extent, deviation, bound, cuts=(), kind=jnp.bfloat16):
    drawn = jax.random.normal(own_key, extent, jnp.float32) * deviation
    if len(cuts) > 0:
        drawn = steps_of(own_key, extent, cuts, -0.22, 0.18) * drawn
    return jnp.clip(drawn, min=-bound, max=bound).astype(kind)


def setup_inputs(seed: int = 0) -> dict:
    key_of = jax.random.split(jax.random.key(seed), 8)
    return {
        "latents": gaussian(key_of[0], (FRAMES, TOK, D), 1.0, 6.0, ((0, 32), (1, 8))),
        "merge_slot": draw_merge_slot(jax.random.fold_in(key_of[7], 71), 0),
        "modulation": gaussian(key_of[2], (6, D), 0.5, 3.0, (), jnp.float32),
        "spatial_qkv": draw_spatial_qkv(jax.random.fold_in(key_of[7], 71), 0),
        "spatial_proj": gaussian(key_of[4], (INNER, D), INNER ** -0.5, 0.25),
        "temporal_qkv": draw_temporal_qkv(jax.random.fold_in(key_of[7], 71), 0),
        "temporal_proj": gaussian(key_of[6], (INNER, D), INNER ** -0.5, 0.25),
    }


def layer_norm(values):
    values = values.astype(jnp.float32)
    center = values - lax.optimization_barrier(jnp.mean(values, -1, keepdims=True))
    spread = lax.optimization_barrier(jnp.mean(center * center, -1, keepdims=True))
    return center * lax.rsqrt(spread + 1e-06)

def modulate(values, modulation, which):
    return (layer_norm(values) * (1.0 + modulation[which + 1]) + modulation[which]).astype(jnp.bfloat16)

def head_attention(operands):
    query_rows, key_rows, value_rows = operands
    scores = jnp.dot(query_rows, key_rows.T, preferred_element_type=jnp.float32) / math.sqrt(HD)
    weights = jnp.exp(scores - lax.optimization_barrier(jnp.max(scores, -1, keepdims=True)))
    row_total = lax.optimization_barrier(jnp.sum(weights, -1, keepdims=True))
    mixture = jnp.dot(weights.astype(jnp.bfloat16), value_rows, preferred_element_type=jnp.float32)
    return (mixture / row_total).astype(jnp.bfloat16)

def by_heads(block):
    return block.reshape(block.shape[0], HEADS, HD).transpose(1, 0, 2)

def reference(latents, merge_slot, modulation, spatial_qkv, spatial_proj, temporal_qkv, temporal_proj):

    def spatial_frame(operands):
        frame_rows, frame_slots = operands
        normed = modulate(frame_rows, modulation, 0)
        one_hot = (frame_slots[:, None] == jnp.arange(HALF, dtype=jnp.int32)[None, :]).astype(jnp.bfloat16)
        counts = lax.optimization_barrier(jnp.sum(one_hot.astype(jnp.float32), 0))
        summed = jnp.dot(one_hot.T, normed, preferred_element_type=jnp.float32)
        merged = (summed / counts[:, None]).astype(jnp.bfloat16)
        projected = jnp.dot(merged, spatial_qkv, preferred_element_type=jnp.float32).astype(jnp.bfloat16)
        heads_out = lax.map(head_attention, (by_heads(projected[:, :INNER]), by_heads(projected[:, INNER:2 * INNER]), by_heads(projected[:, 2 * INNER:])))
        attended = heads_out.transpose(1, 0, 2).reshape(HALF, INNER)
        spatial_out = jnp.dot(attended, spatial_proj, preferred_element_type=jnp.float32).astype(jnp.bfloat16)
        spread_back = jnp.dot(one_hot, spatial_out, preferred_element_type=jnp.float32)
        return (frame_rows.astype(jnp.float32) + modulation[2] * spread_back).astype(jnp.bfloat16)
    after_spatial = lax.map(spatial_frame, (latents, merge_slot))
    by_place = after_spatial.transpose(1, 0, 2).reshape(TOK // ROWS, ROWS, FRAMES, D)

    def temporal_block(block):
        flat = block.reshape(ROWS * FRAMES, D)
        normed = modulate(flat, modulation, 3)
        projected = jnp.dot(normed, temporal_qkv, preferred_element_type=jnp.float32).astype(jnp.bfloat16)
        split = projected.reshape(ROWS, FRAMES, 3, HEADS, HD).astype(jnp.float32)
        scores = jnp.einsum('pfhd,pghd->phfg', split[:, :, 0], split[:, :, 1]) / math.sqrt(HD)
        weights = jnp.exp(scores - lax.optimization_barrier(jnp.max(scores, -1, keepdims=True)))
        row_total = lax.optimization_barrier(jnp.sum(weights, -1))
        rounded = lax.optimization_barrier(weights.astype(jnp.bfloat16)).astype(jnp.float32)
        mixture = jnp.einsum('phfg,pghd->pfhd', rounded, split[:, :, 2]) / row_total.transpose(0, 2, 1)[..., None]
        attended = mixture.astype(jnp.bfloat16).reshape(ROWS * FRAMES, INNER)
        branch = jnp.dot(attended, temporal_proj, preferred_element_type=jnp.float32)
        return (flat.astype(jnp.float32) + modulation[5] * branch).astype(jnp.bfloat16).reshape(ROWS, FRAMES, D)
    finished = lax.map(temporal_block, by_place)
    return finished.reshape(TOK, FRAMES, D).transpose(1, 0, 2)
```

```python
import math

import jax
import jax.numpy as jnp
from jax import lax
from jax.experimental import pallas as pl
from jax.experimental.pallas import tpu as pltpu
from jax.sharding import PartitionSpec as P

MESH = pl.DeviceIdType.MESH
D, HEADS, HD, ROWS, INNER, FRAMES, MROWS = 1152, 8, 72, 448, 576, 32, 224
ALLM = MROWS * HEADS
LOCS = 16
OWNED = FRAMES * LOCS
WIDE = 640
PACK = 256
OROW = 80
LOG2E_SCALE = math.log2(math.e) / math.sqrt(HD)
BF, F32, I32 = jnp.bfloat16, jnp.float32, jnp.int32


def iota(shape, dim):
    return lax.broadcasted_iota(I32, shape, dim)


def onehot(cond):
    return jnp.where(cond, 1.0, 0.0).astype(BF)


def dot(a, b):
    return jnp.dot(a, b, preferred_element_type=F32)


def dot_t(a, b):
    return lax.dot_general(a, b, (((1,), (1,)), ((), ())), preferred_element_type=F32)


def norm_rows(values, scale, shift):
    values = values.astype(F32)
    center = values - jnp.mean(values, -1, keepdims=True)
    spread = jnp.mean(center * center, -1, keepdims=True)
    return (center * lax.rsqrt(spread + 1e-06) * (1.0 + scale) + shift).astype(BF)


def kernel(
    slot_ref, mod_ref, lat_hbm, wsp_hbm, psp_hbm, wt_hbm, pt_hbm, out_hbm,
    lat, wsp, psp, wt, pt, normed, lat_got, lat_perm, qkv_send, qkv_got, keys, att_send, att_got,
    exp_send, exp_got, after, att_perm, ret_send, ret_got, outv, perm, unperm,
    ld_sem, lat_ss, lat_rs, qkv_ss, qkv_rs, att_ss, att_rs, exp_ss, exp_rs, ret_ss, ret_rs, out_sem,
):
    mf = lax.axis_index("frames")
    ms = lax.axis_index("space")
    my, mp = mf // 8, mf % 8
    mz, mx = mp // 4, mp % 4
    mzh, mcore = ms // 2, ms % 2

    def skipped(y):
        return ((y + mcore) % 2) * 4 + (y + 2 * mcore) % 4

    def owns(y, p):
        return p != skipped(y)

    def place(y, p):
        return y * 7 + p - jnp.where(p > skipped(y), 1, 0)

    me_owns = owns(my, mp)
    my_place = place(my, mp)

    def frame_peer(k):
        y = (my + k // 8) % 4
        p = ((mz + (k // 4) % 2) % 2) * 4 + (mx + k % 4) % 4
        return y, p

    def space_peer(k):
        kk = k // 2
        dz = jnp.where(kk == 2, 3, jnp.where(kk == 3, 0, 2 - kk))
        return 2 * ((mzh + dz) % 4) + (mcore + k % 2 + 1) % 2

    def local(src, dst, sem):
        return pltpu.make_async_copy(src, dst, sem)

    def remote(src, dst, ss, rs, f, s):
        return pltpu.make_async_remote_copy(
            src_ref=src, dst_ref=dst, send_sem=ss, recv_sem=rs, device_id=(f, s), device_id_type=MESH
        )

    def rows(ref, start, size, mult):
        return ref.at[pl.ds(pl.multiple_of(start, mult), size)]

    loads = [
        local(src, dst, ld_sem.at[n])
        for n, (src, dst) in enumerate(((lat_hbm, lat), (wsp_hbm, wsp), (psp_hbm, psp), (wt_hbm, wt), (pt_hbm, pt)))
    ]
    loads[0].start()
    barrier = pltpu.get_barrier_semaphore()

    def greet_frame(k, c):
        y, p = frame_peer(k)
        pl.semaphore_signal(barrier, inc=1, device_id=(y * 8 + p, ms), device_id_type=MESH)
        return c

    def greet_space(k, c):
        pl.semaphore_signal(barrier, inc=1, device_id=(mf, (ms + k) % 8), device_id_type=MESH)
        return c

    lax.fori_loop(1, FRAMES, greet_frame, 0)
    lax.fori_loop(1, HEADS, greet_space, 0)
    for copy in loads[1:]:
        copy.start()

    loads[0].wait()

    def norm_chunk(n, c):
        at = pl.ds(pl.multiple_of(n * 64, 64), 64)
        normed[at, :] = norm_rows(lat[at, :], mod_ref[1:2, :], mod_ref[0:1, :])
        return c

    lax.fori_loop(0, ROWS // 64, norm_chunk, 0)
    pl.semaphore_wait(barrier, FRAMES - 1 + HEADS - 1)

    def to_owners(src, got, ss, rs):
        def send(k, c):
            y, p = frame_peer(k)

            @pl.when(owns(y, p))
            def _():
                remote(
                    rows(src, place(y, p) * LOCS, LOCS, LOCS), rows(got, mf * LOCS, LOCS, LOCS),
                    ss, rs, y * 8 + p, ms,
                ).start()

            return c

        @pl.when(me_owns)
        def _():
            local(rows(src, my_place * LOCS, LOCS, LOCS), rows(got, mf * LOCS, LOCS, LOCS), rs).start()

        lax.fori_loop(1, FRAMES, send, 0)

    def drain_to_owners(src, ss):
        @pl.when(me_owns)
        def _():
            part = src.at[pl.ds(0, ROWS - LOCS)]
            local(part, part, ss).wait()

        @pl.when(jnp.logical_not(me_owns))
        def _():
            local(src, src, ss).wait()

    to_owners(lat, lat_got, lat_ss, lat_rs)

    slots = slot_ref[...] - ms * MROWS
    joins = iota((MROWS, ROWS), 0) == slots
    join_t = onehot(joins)
    counts = jnp.sum(jnp.where(joins, 1.0, 0.0), -1, keepdims=True)
    merged = (dot(join_t, normed[...]) / counts).astype(BF)
    loads[1].wait()
    proj = dot(merged, wsp[...]).astype(BF)
    tail = jnp.where(iota((MROWS, PACK - 3 * HD), 1) == 0, 1.0, 0.0).astype(BF)
    for h in range(HEADS):
        qkv_send[h * MROWS : (h + 1) * MROWS, :] = jnp.concatenate(
            [proj[:, n * INNER + h * HD : n * INNER + (h + 1) * HD] for n in range(3)] + [tail], 1
        )

    def send_qkv(k, c):
        s = space_peer(k)

        @pl.when(s != ms)
        def _():
            remote(
                rows(qkv_send, s * MROWS, MROWS, MROWS), rows(qkv_got, ms * MROWS, MROWS, MROWS),
                qkv_ss.at[s], qkv_rs.at[ms], mf, s,
            ).start()

        return c

    lax.fori_loop(0, HEADS, send_qkv, 0)
    local(rows(qkv_send, ms * MROWS, MROWS, MROWS), rows(qkv_got, ms * MROWS, MROWS, MROWS), qkv_rs.at[ms]).start()

    r, c = iota((OWNED, OWNED), 0), iota((OWNED, OWNED), 1)
    perm[...] = onehot((r // FRAMES == c % LOCS) & (r % FRAMES == c // LOCS))
    unperm[...] = onehot((c // FRAMES == r % LOCS) & (c % FRAMES == r // LOCS))
    join = dot_t(onehot(iota((ROWS, ROWS), 0) == iota((ROWS, ROWS), 1)), join_t).astype(BF)
    shift = onehot((iota((PACK, PACK), 0) == iota((PACK, PACK), 1) + HD) & (iota((PACK, PACK), 1) < HD))
    pick = onehot((iota((OROW, PACK), 0) + 2 * HD == iota((OROW, PACK), 1)) & (iota((OROW, PACK), 0) < HD))
    cr, cc = iota((INNER, HEADS * OROW), 0), iota((INNER, HEADS * OROW), 1)
    compact = onehot((cr // HD) * OROW + cr % HD == cc)
    exp_send[:, INNER:] = jnp.zeros((ROWS, WIDE - INNER), BF)
    att_send[...] = jnp.zeros((HEADS * OROW, PACK), BF)

    @pl.when(me_owns)
    def _():
        local(lat_got, lat_got, lat_rs).wait()
        lat_perm[...] = dot(perm[...], lat_got[...]).astype(BF)

    def take_qkv(k, c):
        part = rows(qkv_got, k * MROWS, MROWS, MROWS)
        local(part, part, qkv_rs.at[k]).wait()
        at = pl.ds(pl.multiple_of(k * MROWS, MROWS), MROWS)
        keys[at, :] = dot(qkv_got[at, :], shift).astype(BF)
        return c

    lax.fori_loop(0, HEADS, take_qkv, 0)

    def attend(k, c):
        s = space_peer(k)
        q = qkv_got[pl.ds(pl.multiple_of(s * MROWS, MROWS), MROWS), :]
        scores = dot_t(q, keys[...])
        peak = jnp.max(scores, -1, keepdims=True)
        weights = jnp.exp2((scores - peak) * LOG2E_SCALE).astype(BF)
        mixed = dot(weights, qkv_got[...])
        mixed = (mixed / mixed[:, 3 * HD : 3 * HD + 1]).astype(BF)
        att_send[pl.ds(pl.multiple_of(s * OROW, OROW), OROW), 0:MROWS] = dot_t(pick, mixed).astype(BF)

        @pl.when(s != ms)
        def _():
            remote(
                rows(att_send, s * OROW, OROW, OROW), rows(att_got, ms * OROW, OROW, OROW),
                att_ss.at[s], att_rs.at[ms], mf, s,
            ).start()

        @pl.when(s == ms)
        def _():
            local(rows(att_send, ms * OROW, OROW, OROW), rows(att_got, ms * OROW, OROW, OROW), att_rs.at[ms]).start()

        return c

    lax.fori_loop(0, HEADS, attend, 0)

    def take_att(k, c):
        part = rows(att_got, k * OROW, OROW, OROW)
        local(part, part, att_rs.at[k]).wait()
        return c

    lax.fori_loop(0, HEADS, take_att, 0)
    attended = dot(compact, att_got[:, 0:MROWS]).astype(BF)
    exp_send[:, 0:INNER] = dot_t(join, attended).astype(BF)
    to_owners(exp_send, exp_got, exp_ss, exp_rs)
    loads[2].wait()

    def own_after(n, c):
        at = pl.ds(pl.multiple_of(n * MROWS, MROWS), MROWS)
        branch = dot(exp_send[at, 0:INNER], psp[...]).astype(BF).astype(F32)
        after[at, :] = (lat[at, :].astype(F32) + mod_ref[2:3, :] * branch).astype(BF)
        return c

    lax.fori_loop(0, 2, own_after, 0)
    loads[3].wait()
    loads[4].wait()

    @pl.when(me_owns)
    def _():
        local(exp_got, exp_got, exp_rs).wait()
        near = iota((128, 128), 0) // FRAMES == iota((128, 128), 1) // FRAMES

        def chunk(n, c):
            at = pl.ds(pl.multiple_of(n * 256, 256), 256)
            mine = dot(perm[at, :], exp_got[:, 0:INNER]).astype(BF)
            branch = dot(mine, psp[...]).astype(BF).astype(F32)
            tokens = (lat_perm[at, :].astype(F32) + mod_ref[2:3, :] * branch).astype(BF)
            tokens = norm_rows(tokens, mod_ref[4:5, :], mod_ref[3:4, :])
            inner = dot(tokens, wt[...]).astype(BF)
            for b in range(2):
                part = inner[b * 128 : (b + 1) * 128]
                q, k, v = (part[:, i * INNER : (i + 1) * INNER] for i in range(3))
                tiles = [None] * 5
                for pair in range(4):
                    base = pair * 128
                    width = min(256, INNER - base)
                    lane = iota((128, width), 1) + base
                    total = jnp.zeros((128, width), F32)
                    for h in (2 * pair, 2 * pair + 1):
                        own = (lane >= h * HD) & (lane < (h + 1) * HD)
                        qh = jnp.where(own, q[:, base : base + width].astype(F32), 0.0).astype(BF)
                        scores = jnp.where(near, dot_t(qh, k[:, base : base + width]), -1e30)
                        peak = jnp.max(scores, -1, keepdims=True)
                        weights = jnp.exp2((scores - peak) * LOG2E_SCALE)
                        row_total = jnp.sum(weights, -1, keepdims=True)
                        mixed = dot(weights.astype(BF), v[:, base : base + width])
                        total = jnp.where(own, mixed / row_total, total)
                    for t, piece in ((pair, total[:, :128]), (pair + 1, total[:, 128:])):
                        tiles[t] = piece if tiles[t] is None else tiles[t] + piece
                dst = pl.ds(pl.multiple_of(n * 256 + b * 128, 128), 128)
                for t in range(4):
                    att_perm[dst, t * 128 : (t + 1) * 128] = tiles[t].astype(BF)
                att_perm[dst, 512:INNER] = tiles[4].astype(BF)
            return c

        lax.fori_loop(0, 2, chunk, 0)

        def unpermute(n, c):
            at = pl.ds(pl.multiple_of(n * 256, 256), 256)
            ret_send[at, 0:INNER] = dot(unperm[at, :], att_perm[:, 0:INNER]).astype(BF)
            ret_send[at, INNER:] = jnp.zeros((256, WIDE - INNER), BF)
            return c

        lax.fori_loop(0, 2, unpermute, 0)

        def send_back(k, c):
            y, p = frame_peer(k)
            f = y * 8 + p
            remote(
                rows(ret_send, f * LOCS, LOCS, LOCS), rows(ret_got, my_place * LOCS, LOCS, LOCS),
                ret_ss, ret_rs, f, ms,
            ).start()
            return c

        local(rows(ret_send, mf * LOCS, LOCS, LOCS), rows(ret_got, my_place * LOCS, LOCS, LOCS), ret_rs).start()
        lax.fori_loop(1, FRAMES, send_back, 0)

    local(ret_got, ret_got, ret_rs).wait()

    def finish(n, c):
        at = pl.ds(pl.multiple_of(n * MROWS, MROWS), MROWS)
        branch = dot(ret_got[at, 0:INNER], pt[...])
        outv[at, :] = (after[at, :].astype(F32) + mod_ref[5:6, :] * branch).astype(BF)
        local(outv.at[at], out_hbm.at[at], out_sem.at[n]).start()
        return c

    lax.fori_loop(0, 2, finish, 0)

    drain_to_owners(lat, lat_ss)
    drain_to_owners(exp_send, exp_ss)

    @pl.when(me_owns)
    def _():
        part = ret_send.at[pl.ds(0, OWNED - LOCS)]
        local(part, part, ret_ss).wait()

    def drain_space(k, c):
        s = (ms + k) % 8
        part = rows(qkv_send, s * MROWS, MROWS, MROWS)
        local(part, part, qkv_ss.at[s]).wait()
        part = rows(att_send, s * OROW, OROW, OROW)
        local(part, part, att_ss.at[s]).wait()
        return c

    lax.fori_loop(1, HEADS, drain_space, 0)

    def drain_out(n, c):
        at = pl.ds(pl.multiple_of(n * MROWS, MROWS), MROWS)
        local(outv.at[at], out_hbm.at[at], out_sem.at[n]).wait()
        return c

    lax.fori_loop(0, 2, drain_out, 0)


def shards(latents, merge_slot, modulation, spatial_qkv, spatial_proj, temporal_qkv, temporal_proj):
    vmem = pl.BlockSpec(memory_space=pltpu.VMEM)
    hbm = pl.BlockSpec(memory_space=pl.ANY)
    dma = pltpu.SemaphoreType.DMA
    sizes = (
        (ROWS, D), (D, 3 * INNER), (INNER, D), (D, 3 * INNER), (INNER, D), (ROWS, D), (OWNED, D), (OWNED, D),
        (ALLM, PACK), (ALLM, PACK), (ALLM, PACK), (HEADS * OROW, PACK), (HEADS * OROW, PACK),
        (ROWS, WIDE), (OWNED, WIDE), (ROWS, D), (OWNED, WIDE), (OWNED, WIDE), (ROWS, WIDE), (ROWS, D),
        (OWNED, OWNED), (OWNED, OWNED),
    )
    one = dma(())
    many = dma((HEADS,))
    out = pl.pallas_call(
        kernel,
        out_shape=jax.ShapeDtypeStruct((ROWS, D), BF),
        in_specs=[vmem, vmem] + [hbm] * 5,
        out_specs=hbm,
        scratch_shapes=[pltpu.VMEM(size, BF) for size in sizes]
        + [dma((5,)), one, one, many, many, many, many, one, one, one, one, dma((2,))],
        compiler_params=pltpu.CompilerParams(
            collective_id=0, has_side_effects=True, vmem_limit_bytes=62 * 1024 * 1024
        ),
    )(merge_slot, modulation, latents[0], spatial_qkv, spatial_proj, temporal_qkv, temporal_proj)
    return out[None]


def solution(mesh):
    placed = (P("frames", "space", None), P("frames", "space"), P(), P(), P(), P(), P())
    return jax.shard_map(
        shards, mesh=mesh, in_specs=placed, out_specs=P("frames", "space", None), check_vma=False
    )
```
